32 devices in a mesh: dp: 8 (over y, x, core), seq: 4 (over z).
Axes of the slice: x: 2, y: 2, z: 4, core: 2. Of those that a mesh axis runs over, the one named last changes fastest.
Arguments:
- block_input: bfloat16 [16, 1024, 1024], P('dp', 'seq'), may hold values from -6 to 6
- cotangent: bfloat16 [16, 1024, 1024], P('dp', 'seq'), may hold values from -6 to 6
- in_proj: bfloat16 [1024, 3072], P(('dp', 'seq')), may hold values from -0.1875 to 0.1875
- out_proj: bfloat16 [1024, 1024], P(('dp', 'seq')), may hold values from -0.1875 to 0.1875
- gate_proj: bfloat16 [1024, 4608], P(('dp', 'seq')), may hold values from -0.1875 to 0.1875
- up_proj: bfloat16 [1024, 4608], P(('dp', 'seq')), may hold values from -0.1875 to 0.1875
- down_proj: bfloat16 [4608, 1024], P(('dp', 'seq')), may hold values from -0.09375 to 0.09375
- conv_weight: bfloat16 [1024, 3], P(('dp', 'seq')), may hold values from -3 to 3
- mixer_gain: bfloat16 [1024], P(('dp', 'seq')), may hold values from 0.25 to 1.75
- ffn_gain: bfloat16 [1024], P(('dp', 'seq')), may hold values from 0.25 to 1.75
Outputs:
- block_output: bfloat16 [16, 1024, 1024], P('dp', 'seq')
- input_grad: bfloat16 [16, 1024, 1024], P('dp', 'seq')
- grad_in_proj: float32 [1024, 3072], P(('dp', 'seq'))
- grad_out_proj: float32 [1024, 1024], P(('dp', 'seq'))
- grad_gate_proj: float32 [1024, 4608], P(('dp', 'seq'))
- grad_up_proj: float32 [1024, 4608], P(('dp', 'seq'))
- grad_down_proj: float32 [4608, 1024], P(('dp', 'seq'))
- grad_conv_weight: float32 [1024, 3], P(('dp', 'seq'))
- grad_mixer_gain: float32 [1024], P(('dp', 'seq'))
- grad_ffn_gain: float32 [1024], P(('dp', 'seq'))
The draws below stay inside these ranges and needn't reach their ends.
All inputs are finite; a program needn't handle non-finite values.
Results may differ from the reference program's by a relative error of at most 0.0093.
Values may be sent and summed in bfloat16 or wider, within the bound.
No kernel may reach another device: no remote copies, remote signals or barrier semaphores. Data moves between devices by JAX's collectives and lax.ppermute only.
A program may use at most 192 MiB of HBM per device.

```python
import math
import jax
import jax.numpy as jnp
from jax import lax

D = 1024
FF = 4608
KW = 3
SEQ_LEN = 1024
SEQS = 16


def level_of(own_key, dims, pieces, smallest, high):
    level, own = 1.0, jax.random.fold_in(own_key, 6)
    for dim, shards_of in pieces:
        draws = jnp.exp(jax.random.uniform(jax.random.fold_in(own, dim), (shards_of,), jnp.float32, smallest / len(pieces), high / len(pieces)))
        level = level * jnp.repeat(draws, dims[dim] // shards_of).reshape([-1 if axis == dim else 1 for axis in range(len(dims))])
    return level


def centred(own_key, extent, spread, reach, cuts=(), dtype=jnp.bfloat16):
    array = jax.random.normal(own_key, extent, jnp.float32) * spread
    if len(cuts) > 0:
        array = level_of(own_key, extent, cuts, -0.22, 0.18) * array
    return jnp.clip(array, min=-reach, max=reach).astype(dtype)


def setup_inputs(seed: int = 0) -> dict:
    key_list = jax.random.split(jax.random.key(seed), 11)
    block_input = centred(key_list[0], (SEQS, SEQ_LEN, D), 1.0, 6.0, ((0, 8), (1, 4)))
    cotangent = centred(key_list[1], (SEQS, SEQ_LEN, D), 1.0, 6.0, ((0, 8), (1, 4)))
    in_proj = centred(key_list[2], (D, 3 * D), D ** -0.5, 0.1875, ((0, 32),))
    out_proj = centred(key_list[3], (D, D), D ** -0.5, 0.1875, ((0, 32),))
    gate_proj = centred(key_list[4], (D, FF), D ** -0.5, 0.1875, ((0, 32),))
    up_proj = centred(key_list[5], (D, FF), D ** -0.5, 0.1875, ((0, 32),))
    down_proj = centred(key_list[6], (FF, D), FF ** -0.5, 0.09375, ((0, 32),))
    conv_weight = centred(key_list[7], (D, KW), 0.5, 3.0, ((0, 32),))
    mixer_gain = jnp.clip(1.0 + 0.15 * jax.random.normal(key_list[8], (D,), jnp.float32), 0.25, 1.75).astype(jnp.bfloat16)
    ffn_gain = jnp.clip(1.0 + 0.15 * jax.random.normal(key_list[9], (D,), jnp.float32), 0.25, 1.75).astype(jnp.bfloat16)
    return dict(block_input=block_input, cotangent=cotangent, in_proj=in_proj, out_proj=out_proj, gate_proj=gate_proj, up_proj=up_proj, down_proj=down_proj, conv_weight=conv_weight, mixer_gain=mixer_gain, ffn_gain=ffn_gain)


epsilon = 1e-05

@jax.custom_vjp
def low(v):
    return lax.optimization_barrier(v.astype(jnp.bfloat16)).astype(jnp.float32)

@jax.custom_vjp
def low_back(v):
    return v

def low_keep(v):
    return (low(v), None)

def low_pass(kept, grad):
    return (grad,)

def back_keep(v):
    return (v, None)

def back_low(kept, grad):
    return (low(grad),)
low.defvjp(low_keep, low_pass)
low_back.defvjp(back_keep, back_low)

def product(first_arg, second_arg):
    return jnp.einsum('gld,de->gle', first_arg, second_arg, precision=lax.Precision.HIGHEST)

def rms_scale(values):
    return lax.rsqrt(lax.optimization_barrier(jnp.mean(values * values, axis=-1, keepdims=True)) + epsilon)

def forward(block_acts, in_proj, out_proj, gate_proj, up_proj, down_proj, conv_weight, mixer_gain, ffn_gain):
    mixer_in = low(block_acts * rms_scale(block_acts) * mixer_gain)
    projected = low_back(product(mixer_in, in_proj))
    b_part = projected[..., :D]
    c_part = projected[..., D:2 * D]
    x_part = projected[..., 2 * D:]
    bx_value = low(b_part * x_part)
    padded = jnp.pad(bx_value, ((0, 0), (KW - 1, 0), (0, 0)))
    conv_out = jnp.zeros_like(bx_value)
    for offset in range(KW):
        conv_out = conv_out + conv_weight[:, offset] * padded[:, offset:offset + SEQ_LEN, :]
    mixed_y = low(c_part * conv_out)
    middle = block_acts + low_back(product(mixed_y, out_proj))
    ffn_in = low(middle * rms_scale(middle) * ffn_gain)
    gate_pre = low_back(product(ffn_in, gate_proj))
    up_value = low_back(product(ffn_in, up_proj))
    hidden = low(jax.nn.silu(gate_pre) * up_value)
    return middle + low_back(product(hidden, down_proj))

def reference(block_input, cotangent, in_proj, out_proj, gate_proj, up_proj, down_proj, conv_weight, mixer_gain, ffn_gain):
    weights_f32 = tuple((weight.astype(jnp.float32) for weight in (in_proj, out_proj, gate_proj, up_proj, down_proj, conv_weight, mixer_gain, ffn_gain)))
    group_size = math.gcd(SEQS, max(1, 4096 // SEQ_LEN))
    blocks_in = block_input.astype(jnp.float32).reshape(SEQS // group_size, group_size, SEQ_LEN, D)
    blocks_grad = cotangent.astype(jnp.float32).reshape(SEQS // group_size, group_size, SEQ_LEN, D)

    def scan_step(running_sums, block_pair):
        outputs_now, pullback = jax.vjp(forward, block_pair[0], *weights_f32)
        gradients = pullback(block_pair[1])
        running_sums = tuple((running + gradient for running, gradient in zip(running_sums, gradients[1:])))
        return (running_sums, (outputs_now.astype(jnp.bfloat16), gradients[0].astype(jnp.bfloat16)))
    initial = tuple((jnp.zeros(weight.shape, jnp.float32) for weight in weights_f32))
    running_sums, (outputs_all, input_grads) = lax.scan(scan_step, initial, (blocks_in, blocks_grad))
    return (outputs_all.reshape(SEQS, SEQ_LEN, D), input_grads.reshape(SEQS, SEQ_LEN, D), running_sums[0], running_sums[1], running_sums[2], running_sums[3], running_sums[4], running_sums[5], running_sums[6], running_sums[7])
```

```python
import jax
import jax.numpy as jnp
from jax import lax
from jax.sharding import PartitionSpec as P

epsilon = 1e-05
LOW = jnp.bfloat16
F32 = jnp.float32
SMALL = 128


def along_seq(value, steps):
    count = lax.axis_size("seq")
    leading, last = (max(0, -steps), min(count, count - steps))
    return lax.ppermute(value, "seq", [(source, source + steps) for source in range(leading, last)])


def swap(value, mask):
    count = lax.axis_size("dp")
    return lax.ppermute(value, "dp", [(source, source ^ mask) for source in range(count)])


def dot(a, b, a_dim, b_dim, out=F32):
    return lax.dot_general(
        a, b, (((a_dim,), (b_dim,)), ((), ())), preferred_element_type=F32
    ).astype(out)


def norm_back(grad_normed, normed, scale, gain):
    grad_scaled = grad_normed * gain
    return scale * (grad_scaled - normed * jnp.mean(grad_scaled * normed, axis=-1, keepdims=True))


def xor_order(stack, index):
    count = stack.shape[0]
    return jnp.stack(
        [lax.dynamic_index_in_dim(stack, j ^ index, 0, keepdims=False) for j in range(count)]
    )


def xor_columns(value, index, count):
    width = value.shape[1] // count
    rows = value.shape[0]
    return jnp.concatenate(
        [lax.dynamic_slice(value, (0, (j ^ index) * width), (rows, width)) for j in range(count)],
        axis=1,
    )


def spread(own, masks):
    pieces = [own]
    for mask in masks:
        held = pieces[0] if len(pieces) == 1 else jnp.concatenate(pieces, axis=0)
        pieces.append(swap(held, mask))
    return pieces


def rel_sets(masks):
    sets, held = [[0]], [0]
    for mask in masks:
        new = [j ^ mask for j in held]
        sets.append(new)
        held = held + new
    return sets


def blocks_in_order(pieces, masks, rows):
    found = {}
    for piece, members in zip(pieces, rel_sets(masks)):
        for place, member in enumerate(members):
            found[member] = piece[place * rows : (place + 1) * rows]
    return jnp.concatenate([found[j] for j in range(len(found))], axis=0)


def collect(blocks, masks):
    sets = rel_sets(masks)
    held = dict(blocks)
    for level in range(len(masks), 0, -1):
        mask = masks[level - 1]
        kept = [j for members in sets[:level] for j in members]
        sent = jnp.concatenate([held[j ^ mask] for j in kept], axis=0)
        got = swap(sent, mask)
        rows = sent.shape[0] // len(kept)
        held = {
            j: (held[j].astype(F32) + got[i * rows : (i + 1) * rows].astype(F32)).astype(LOW)
            for i, j in enumerate(kept)
        }
    return held[0]


def shards(
    block_input,
    cotangent,
    in_proj,
    out_proj,
    gate_proj,
    up_proj,
    down_proj,
    conv_weight,
    mixer_gain,
    ffn_gain,
):
    nd, ns = lax.axis_size("dp"), lax.axis_size("seq")
    chips = nd // 2
    me = lax.axis_index("dp")
    chip, core = me // 2, me % 2
    bits = []
    while 2 ** len(bits) < chips:
        bits.append(2 << len(bits))
    seqs, span, width = block_input.shape
    rows_all = seqs * span
    own_rows = in_proj.shape[0]
    block_rows = own_rows * ns
    taps = conv_weight.shape[1]
    halo = taps - 1
    slice_ff = gate_proj.shape[1] // chips

    small = jnp.concatenate([conv_weight, mixer_gain[:, None], ffn_gain[:, None]], axis=1)
    small = jnp.pad(small, ((0, 0), (0, SMALL - small.shape[1])))
    packed = jnp.concatenate([in_proj, out_proj, small], axis=1)
    packed = lax.all_gather(packed, "seq", axis=0, tiled=True)
    order_one = bits + [1]
    order_two = bits[::-1] + [1]
    pieces_one = spread(packed[:, : 2 * width], order_one)
    pieces_two = spread(packed[:, 2 * width :], order_two)
    mix_one = blocks_in_order(pieces_one, order_one, block_rows)
    mix_two = blocks_in_order(pieces_two, order_two, block_rows)
    in_bc, in_x = mix_one, mix_two[:, :width]
    out_w = mix_two[:, width : 2 * width]
    small_rel = mix_two[:, 2 * width :].astype(F32)[:, : taps + 2]
    small_nat = xor_order(small_rel.reshape(nd, block_rows, taps + 2), me).reshape(width, taps + 2)
    conv_taps = [small_nat[:, j] for j in range(taps)]
    gain_one, gain_two = small_nat[:, taps], small_nat[:, taps + 1]

    def columns_for(mask):
        at = (chip ^ mask) * slice_ff
        return jnp.concatenate(
            [
                lax.dynamic_slice(w, (0, at), (own_rows, slice_ff))
                for w in (gate_proj, up_proj)
            ],
            axis=1,
        )

    gate_up = jnp.stack(
        [columns_for(0)] + [swap(columns_for(k), 2 * k) for k in range(1, chips)]
    )
    gate_up = xor_order(gate_up, chip)
    gate_up = lax.all_gather(gate_up, "seq", axis=0, tiled=False)
    other = swap(gate_up, 1)
    gate_up, other = (v.transpose(1, 0, 2, 3) for v in (gate_up, other))
    gate_up = jnp.stack(
        [jnp.where(core == 0, gate_up, other), jnp.where(core == 0, other, gate_up)], axis=1
    ).reshape(width, 2 * slice_ff)
    down = lax.all_gather(down_proj, "seq", axis=0, tiled=True)
    other = swap(down, 1)
    down = jnp.concatenate(
        [jnp.where(core == 0, down, other), jnp.where(core == 0, other, down)], axis=0
    )

    residual = block_input.astype(F32).reshape(rows_all, width)
    scale_one = lax.rsqrt(jnp.mean(residual * residual, axis=-1, keepdims=True) + epsilon)
    normed_one = residual * scale_one
    mixer_in = (normed_one * gain_one).astype(LOW)
    mixer_rel = xor_columns(mixer_in, me, nd)
    projected = dot(mixer_rel, in_bc, 1, 0)
    b_part = projected[:, :width]
    c_part = projected[:, width:]
    x_part = dot(mixer_rel, in_x, 1, 0)
    bx_value = (b_part * x_part).astype(LOW).reshape(seqs, span, width)
    tail_rows = along_seq(bx_value[:, span - halo :, :], 1)
    extended = jnp.concatenate([tail_rows, bx_value], axis=1)
    conv_out = jnp.zeros((seqs, span, width), F32)
    for j in range(taps):
        conv_out = conv_out + conv_taps[j] * extended[:, j : j + span, :].astype(F32)
    conv_flat = conv_out.reshape(rows_all, width)
    mixed_y = (c_part * conv_flat).astype(LOW)
    mixed_rel = xor_columns(mixed_y, me, nd)
    middle = residual + dot(mixed_rel, out_w, 1, 0)
    scale_two = lax.rsqrt(jnp.mean(middle * middle, axis=-1, keepdims=True) + epsilon)
    normed_two = middle * scale_two
    ffn_in = (normed_two * gain_two).astype(LOW)

    half = rows_all // 2
    orders = (bits, bits[::-1])
    out_grad = cotangent.reshape(rows_all, width)

    def gathered(value):
        found = [
            spread(value[i * half : (i + 1) * half], order) for i, order in enumerate(orders)
        ]
        chunks = [jnp.concatenate([found[0][0], found[0][1], found[1][0], found[1][1]], axis=0)]
        for level in range(2, len(bits) + 1):
            chunks.append(jnp.concatenate([found[0][level], found[1][level]], axis=0))
        return chunks

    grads_chunks = gathered(out_grad)
    acts_chunks = gathered(ffn_in)
    hidden, grad_gu = [], []
    for acts, grads in zip(acts_chunks, grads_chunks):
        gate_pre = dot(acts, gate_up[:, :slice_ff], 1, 0)
        up_value = dot(acts, gate_up[:, slice_ff:], 1, 0)
        grad_hidden = dot(grads, down, 1, 1)
        sig = jax.nn.sigmoid(gate_pre)
        silu = gate_pre * sig
        hidden.append((silu * up_value).astype(LOW))
        grad_gate = (grad_hidden * up_value * sig * (1.0 + gate_pre * (1.0 - sig))).astype(LOW)
        grad_up = (grad_hidden * silu).astype(LOW)
        grad_gu.append(jnp.concatenate([grad_gate, grad_up], axis=1))

    def summed_to_owner(parts):
        parts = list(parts)
        for level in range(len(bits), 1, -1):
            part = parts[level - 1]
            cut = part.shape[0] // 2
            got = [swap(part[:cut], orders[0][level - 1]), swap(part[cut:], orders[1][level - 1])]
            lower = [p for p in parts[: level - 1]]
            for color in (0, 1):
                at = 0
                for i, p in enumerate(lower):
                    n = p.shape[0] // 2
                    piece = p[color * n : (color + 1) * n].astype(F32) + got[color][
                        at : at + n
                    ].astype(F32)
                    at += n
                    lower[i] = (
                        jnp.concatenate([piece, p[n:].astype(F32)], axis=0)
                        if color == 0
                        else jnp.concatenate([p[:n].astype(F32), piece], axis=0)
                    )
            parts = [p.astype(LOW) for p in lower]
        first = parts[0]
        got = [
            swap(first[half : 2 * half], orders[0][0]),
            swap(first[3 * half : 4 * half], orders[1][0]),
        ]
        return jnp.concatenate(
            [
                first[:half].astype(F32) + got[0].astype(F32),
                first[2 * half : 3 * half].astype(F32) + got[1].astype(F32),
            ],
            axis=0,
        )

    grad_norm_two = summed_to_owner([dot(g, gate_up, 1, 1, LOW) for g in grad_gu][: len(grad_gu)])
    down_term = summed_to_owner([dot(h, down, 1, 0, LOW) for h in hidden])
    block_output = (middle + down_term).astype(LOW).reshape(seqs, span, width)

    grad_gate_up = sum(dot(a, g, 0, 0) for a, g in zip(acts_chunks, grad_gu)).astype(LOW)
    grad_gate_up = grad_gate_up.reshape(chips, 2, ns, own_rows, 2 * slice_ff)
    keep = lax.dynamic_index_in_dim(grad_gate_up, core, 1, keepdims=False)
    send = lax.dynamic_index_in_dim(grad_gate_up, 1 - core, 1, keepdims=False)
    total = (keep.astype(F32) + swap(send, 1).astype(F32)).astype(LOW).transpose(1, 0, 2, 3)
    total = lax.psum_scatter(total, "seq", scatter_dimension=0, tiled=False)

    def rows_for(mask):
        return lax.dynamic_index_in_dim(total, chip ^ mask, 0, keepdims=False)

    owned = jnp.stack([rows_for(0)] + [swap(rows_for(k), 2 * k) for k in range(1, chips)])
    owned = xor_order(owned, chip).astype(F32).transpose(1, 0, 2)
    grad_gate_w = owned[:, :, :slice_ff].reshape(own_rows, chips * slice_ff)
    grad_up_w = owned[:, :, slice_ff:].reshape(own_rows, chips * slice_ff)

    grad_down = sum(dot(h, g, 0, 0) for h, g in zip(hidden, grads_chunks)).astype(LOW)
    grad_down = grad_down.reshape(2, slice_ff // 2, width)
    keep = lax.dynamic_index_in_dim(grad_down, core, 0, keepdims=False)
    send = lax.dynamic_index_in_dim(grad_down, 1 - core, 0, keepdims=False)
    total_down = (keep.astype(F32) + swap(send, 1).astype(F32)).astype(LOW)
    grad_down_w = lax.psum_scatter(total_down, "seq", scatter_dimension=0, tiled=True).astype(F32)

    grad_ffn_gain = jnp.sum(grad_norm_two * normed_two, axis=0)
    grad_middle = out_grad.astype(F32) + norm_back(grad_norm_two, normed_two, scale_two, gain_two)
    grad_mid_low = grad_middle.astype(LOW)
    grad_out_w = dot(mixed_rel, grad_mid_low, 0, 0, LOW)
    grad_y = xor_columns(dot(grad_mid_low, out_w, 1, 1), me, nd)
    grad_c = grad_y * conv_flat
    grad_conv = (grad_y * c_part).reshape(seqs, span, width)
    head_rows = along_seq(grad_conv[:, :halo, :].astype(LOW), -1).astype(F32)
    grad_ext = jnp.concatenate([grad_conv, head_rows], axis=1)
    grad_bx = jnp.zeros((seqs, span, width), F32)
    tap_grads = []
    for j in range(taps):
        start_at = halo - j
        grad_bx = grad_bx + conv_taps[j] * grad_ext[:, start_at : start_at + span, :]
        tap_grads.append(
            jnp.sum(grad_conv * extended[:, j : j + span, :].astype(F32), axis=(0, 1))
        )
    grad_bx = grad_bx.reshape(rows_all, width)
    grad_bc = jnp.concatenate([grad_bx * x_part, grad_c], axis=1).astype(LOW)
    grad_x = (grad_bx * b_part).astype(LOW)
    grad_in_bc = dot(mixer_rel, grad_bc, 0, 0, LOW)
    grad_in_x = dot(mixer_rel, grad_x, 0, 0, LOW)
    grad_norm_one = xor_columns(
        dot(grad_bc, in_bc, 1, 1) + dot(grad_x, in_x, 1, 1), me, nd
    )
    grad_mix_gain = jnp.sum(grad_norm_one * normed_one, axis=0)
    input_grad = grad_middle + norm_back(grad_norm_one, normed_one, scale_one, gain_one)
    input_grad = input_grad.astype(LOW).reshape(seqs, span, width)

    small_grad = jnp.stack(tap_grads + [grad_mix_gain, grad_ffn_gain], axis=1)
    small_grad = xor_order(small_grad.reshape(nd, block_rows, taps + 2), me)
    small_grad = jnp.pad(
        small_grad.reshape(width, taps + 2), ((0, 0), (0, SMALL - taps - 2))
    ).astype(LOW)
    grad_two = jnp.concatenate([grad_in_x, grad_out_w, small_grad], axis=1)

    def by_block(value):
        return {j: value[j * block_rows : (j + 1) * block_rows] for j in range(nd)}

    mine = jnp.concatenate(
        [collect(by_block(grad_in_bc), order_one), collect(by_block(grad_two), order_two)], axis=1
    )
    mine = lax.psum_scatter(mine, "seq", scatter_dimension=0, tiled=True).astype(F32)
    return (
        block_output,
        input_grad,
        mine[:, : 3 * width],
        mine[:, 3 * width : 4 * width],
        grad_gate_w,
        grad_up_w,
        grad_down_w,
        mine[:, 4 * width : 4 * width + taps],
        mine[:, 4 * width + taps],
        mine[:, 4 * width + taps + 1],
    )


def solution(mesh):
    rows, vector = P(("dp", "seq"), None), P(("dp", "seq"))
    acts = P("dp", "seq", None)
    in_specs = (acts, acts) + (rows,) * 6 + (vector,) * 2
    out_specs = (acts, acts) + (rows,) * 6 + (vector,) * 2
    return jax.shard_map(shards, mesh=mesh, in_specs=in_specs, out_specs=out_specs, check_vma=False)
```

```python
import functools

import jax
import jax.numpy as jnp
from jax import lax
from jax.experimental import pallas as pl
from jax.experimental.pallas import tpu as pltpu
from jax.sharding import PartitionSpec as P


epsilon = 1e-05
LOW = jnp.bfloat16
F32 = jnp.float32
SMALL = 128
VMEM_LIMIT = 60 * 1024 * 1024


def along_seq(value, steps):
    count = lax.axis_size("seq")
    leading, last = (max(0, -steps), min(count, count - steps))
    return lax.ppermute(value, "seq", [(source, source + steps) for source in range(leading, last)])


def swap(value, mask):
    count = lax.axis_size("dp")
    return lax.ppermute(value, "dp", [(source, source ^ mask) for source in range(count)])


def dot(a, b, a_dim, b_dim, out=F32):
    return lax.dot_general(
        a, b, (((a_dim,), (b_dim,)), ((), ())), preferred_element_type=F32
    ).astype(out)


def norm_back(grad_normed, normed, scale, gain):
    grad_scaled = grad_normed * gain
    return scale * (grad_scaled - normed * jnp.mean(grad_scaled * normed, axis=-1, keepdims=True))


def rms_scale(value):
    return lax.rsqrt(jnp.mean(value * value, axis=-1, keepdims=True) + epsilon)


def xor_order(stack, index):
    count = stack.shape[0]
    return jnp.stack(
        [lax.dynamic_index_in_dim(stack, j ^ index, 0, keepdims=False) for j in range(count)]
    )


def spread(own, masks):
    held = {0: own}
    for mask in masks:
        for j in list(held):
            held[j ^ mask] = swap(held[j], mask)
    return held


def level_sets(masks):
    held = [0, masks[0]]
    sets = [list(held)]
    for mask in masks[1:]:
        new = [j ^ mask for j in held]
        sets.append(new)
        held = held + new
    return sets


def kept_order(masks):
    held = [0]
    for mask in masks:
        held = held + [j ^ mask for j in held]
    return held


def halve(held, mask, *waits):
    rows = held.shape[0] // 2
    got = swap(held[rows:], mask)
    return held[:rows], got


def added(kept, got):
    return (kept.astype(F32) + got.astype(F32)).astype(LOW)


def after(value, *others):
    return lax.optimization_barrier((value,) + others)[0]


def params(**more):
    return pltpu.CompilerParams(vmem_limit_bytes=VMEM_LIMIT, **more)


ANY = pl.BlockSpec(memory_space=pl.ANY)
VMEM = pl.BlockSpec(memory_space=pltpu.VMEM)
SMEM = pl.BlockSpec(memory_space=pltpu.SMEM)


def mixer_in_kernel(count, me_ref, x_ref, *refs):
    blocks = refs[: 2 * count]
    w_out, small_ref, in_ref, b_ref, xp_ref, bx_ref, w, sems, out_sem = refs[2 * count :]
    rows = blocks[0].shape[0]
    cut = blocks[0].shape[1]
    width = x_ref.shape[1]
    me = me_ref[0]
    copies = []
    for j in range(count):
        at = pl.multiple_of((me ^ j) * rows, rows)
        for i, columns in ((0, pl.ds(0, cut)), (1, pl.ds(cut, w.shape[1] - cut))):
            copy = pltpu.make_async_copy(
                blocks[2 * j + i], w.at[pl.ds(at, rows), columns], sems.at[2 * j + i]
            )
            copy.start()
            copies.append(copy)
    x = x_ref[...].astype(F32)
    normed = x * rms_scale(x)
    for copy in copies:
        copy.wait()
    back = pltpu.make_async_copy(w, w_out, out_sem)
    back.start()
    small = w[:, 3 * width :].astype(F32).T[:8]
    small_ref[...] = small
    taps = 3
    mixer_in = (normed * small[taps : taps + 1]).astype(LOW)
    in_ref[...] = mixer_in
    b_part = dot(mixer_in, w[:, :width], 1, 0)
    b_ref[...] = b_part
    x_part = dot(mixer_in, w[:, 2 * width : 3 * width], 1, 0)
    xp_ref[...] = x_part
    bx_ref[...] = (b_part * x_part).astype(LOW)
    back.wait()


def mixer_in_call(me, x, blocks_one, blocks_two):
    count = len(blocks_one)
    rows, width = x.shape
    blocks = [b for j in range(count) for b in (blocks_one[j], blocks_two[j])]
    total = blocks_one[0].shape[1] + blocks_two[0].shape[1]
    f32 = jax.ShapeDtypeStruct((rows, width), F32)
    low = jax.ShapeDtypeStruct((rows, width), LOW)
    return pl.pallas_call(
        functools.partial(mixer_in_kernel, count),
        in_specs=[SMEM, VMEM] + [ANY] * len(blocks),
        out_specs=[ANY] + [VMEM] * 5,
        out_shape=[
            jax.ShapeDtypeStruct((width, total), LOW),
            jax.ShapeDtypeStruct((8, width), F32),
            low,
            f32,
            f32,
            low,
        ],
        scratch_shapes=[
            pltpu.VMEM((width, total), LOW),
            pltpu.SemaphoreType.DMA((2 * count,)),
            pltpu.SemaphoreType.DMA,
        ],
        cost_estimate=pl.CostEstimate(
            flops=4 * rows * width * width, bytes_accessed=4 * width * total, transcendentals=0
        ),
        compiler_params=params(),
        name="mixer_in",
    )(me, x, *blocks)


def mixer_out_kernel(count, seqs, me_ref, x_ref, bx_ref, tail_ref, c_ref, small_ref, *refs):
    blocks = refs[:count]
    w_out, conv_ref, mixed_ref, middle_ref, one_ref, two_ref, w, ext, sems, out_sem = refs[count:]
    rows = blocks[0].shape[0]
    me = me_ref[0]
    copies = []
    for j in range(count):
        at = pl.multiple_of((me ^ j) * rows, rows)
        copy = pltpu.make_async_copy(blocks[j], w.at[pl.ds(at, rows)], sems.at[j])
        copy.start()
        copies.append(copy)
    span = x_ref.shape[0] // seqs
    halo = tail_ref.shape[1]
    taps = halo + 1
    for s in range(seqs):
        part = pl.ds(s * span, span)
        ext[pl.ds(8, span)] = bx_ref[part].astype(F32)
        ext[8 - halo : 8] = tail_ref[s].astype(F32)
        conv = jnp.zeros((span, x_ref.shape[1]), F32)
        for j in range(taps):
            conv = conv + small_ref[j : j + 1] * ext[pl.ds(8 - halo + j, span)]
        conv_ref[part] = conv
        mixed_ref[part] = (c_ref[part] * conv).astype(LOW)
    for copy in copies:
        copy.wait()
    back = pltpu.make_async_copy(w, w_out, out_sem)
    back.start()
    middle = x_ref[...].astype(F32) + dot(mixed_ref[...], w[...], 1, 0)
    middle_ref[...] = middle
    ffn_in = (middle * rms_scale(middle) * small_ref[taps + 1 : taps + 2]).astype(LOW)
    half = x_ref.shape[0] // 2
    one_ref[...] = ffn_in[:half]
    two_ref[...] = ffn_in[half:]
    back.wait()


def mixer_out_call(me, x, bx, tail, c_part, small, blocks):
    count = len(blocks)
    rows, width = x.shape
    seqs = tail.shape[0]
    f32 = jax.ShapeDtypeStruct((rows, width), F32)
    low = jax.ShapeDtypeStruct((rows, width), LOW)
    half = jax.ShapeDtypeStruct((rows // 2, width), LOW)
    return pl.pallas_call(
        functools.partial(mixer_out_kernel, count, seqs),
        in_specs=[SMEM] + [VMEM] * 5 + [ANY] * count,
        out_specs=[ANY] + [VMEM] * 5,
        out_shape=[jax.ShapeDtypeStruct((width, width), LOW), f32, low, f32, half, half],
        scratch_shapes=[
            pltpu.VMEM((width, width), LOW),
            pltpu.VMEM((rows // seqs + 8, width), F32),
            pltpu.SemaphoreType.DMA((count,)),
            pltpu.SemaphoreType.DMA,
        ],
        cost_estimate=pl.CostEstimate(
            flops=2 * rows * width * width, bytes_accessed=8 * width * width, transcendentals=0
        ),
        compiler_params=params(),
        name="mixer_out",
    )(me, x, bx, tail, c_part, small, *[blocks[j] for j in range(count)])


def ffn_kernel(count, kept, w_ref, d_ref, *refs):
    acts, grads = refs[:count], refs[count : 2 * count]
    hid_ref, gu_ref, act_ref, grad_ref, na_ref, nb_ref, da_ref, db_ref, abuf, gbuf, sems = refs[
        2 * count + kept :
    ]
    step = pl.program_id(0)

    def copies(i):
        return (
            pltpu.make_async_copy(acts[i], abuf.at[i], sems.at[0, i]),
            pltpu.make_async_copy(grads[i], gbuf.at[i], sems.at[1, i]),
        )

    @pl.when(step == 0)
    def _():
        for i in range(count):
            for copy in copies(i):
                copy.start()

    for i in range(count):

        @pl.when(step == i)
        def _():
            for copy in copies(i):
                copy.wait()

    act, grad = abuf[step], gbuf[step]
    ff = d_ref.shape[0]
    both = dot(act, w_ref[...], 1, 0)
    grad_hidden = dot(grad, d_ref[...], 1, 1)
    gate_pre, up_value = both[:, :ff], both[:, ff:]
    sig = jax.nn.sigmoid(gate_pre)
    silu = gate_pre * sig
    hidden = (silu * up_value).astype(LOW)
    hid_ref[...] = hidden
    gu_ref[:, :ff] = (grad_hidden * up_value * sig * (1.0 + gate_pre * (1.0 - sig))).astype(LOW)
    gu_ref[:, ff:] = (grad_hidden * silu).astype(LOW)
    act_ref[...] = act
    grad_ref[...] = grad
    norm = dot(gu_ref[...], w_ref[...], 1, 1, LOW)
    down = dot(hidden, d_ref[...], 1, 0, LOW)

    @pl.when(step < count // 2)
    def _():
        na_ref[...] = norm
        da_ref[...] = down

    @pl.when(step >= count // 2)
    def _():
        nb_ref[...] = norm
        db_ref[...] = down


def ffn_call(acts, grads, gate_up, down, kept, base, total):
    count = len(acts)
    rows, width = acts[0].shape
    ff = down.shape[0]
    first = base // rows
    low = functools.partial(jax.ShapeDtypeStruct, dtype=LOW)
    shapes = [(total, ff), (total, 2 * ff), (total, width), (total, width)]
    part = (count // 2 * rows, width)
    lower = pl.BlockSpec((rows, width), lambda i: (jnp.minimum(i, count // 2 - 1), 0))
    upper = pl.BlockSpec((rows, width), lambda i: (jnp.maximum(i - count // 2, 0), 0))
    once = pl.Buffered(1)
    return pl.pallas_call(
        functools.partial(ffn_kernel, count, len(kept)),
        grid=(count,),
        in_specs=[
            pl.BlockSpec((width, 2 * ff), lambda i: (0, 0), pipeline_mode=once),
            pl.BlockSpec((ff, width), lambda i: (0, 0), pipeline_mode=once),
        ]
        + [ANY] * (2 * count + len(kept)),
        out_specs=[pl.BlockSpec((rows, s[1]), lambda i: (first + i, 0)) for s in shapes]
        + [lower, upper, lower, upper],
        out_shape=[low(s) for s in shapes] + [low(part)] * 4,
        input_output_aliases={2 + 2 * count + i: i for i in range(len(kept))},
        scratch_shapes=[
            pltpu.VMEM((count, rows, width), LOW),
            pltpu.VMEM((count, rows, width), LOW),
            pltpu.SemaphoreType.DMA((2, count)),
        ],
        cost_estimate=pl.CostEstimate(
            flops=12 * count * rows * ff * width,
            bytes_accessed=2 * (3 * ff * width + count * rows * (3 * ff + 6 * width)),
            transcendentals=count * rows * ff,
        ),
        compiler_params=params(dimension_semantics=("arbitrary",)),
    )(gate_up, down, *acts, *grads, *kept)


def place_rows(me, kept, scratch, keep_ref, send_ref, sems):
    rows = scratch.shape[0] // (2 * len(kept))
    copies = []
    for i, j in enumerate(kept):
        for k, (member, ref) in enumerate(((j ^ 1, send_ref), (j, keep_ref))):
            at = pl.multiple_of((me ^ member) * rows, rows)
            copy = pltpu.make_async_copy(
                scratch.at[pl.ds(at, rows)], ref.at[pl.ds(i * rows, rows)], sems.at[i, k]
            )
            copy.start()
            copies.append(copy)
    return copies


def mixer_back_kernel(
    one_ref, got_one_ref, two_ref, got_two_ref, cot_ref, middle_ref, small_ref, w_ref, conv_ref,
    c_ref, grad_middle_ref, low_ref, grad_c_ref, grad_conv_ref, gain_ref,
):
    half = got_one_ref.shape[0]
    total = 0.0
    taps = 3
    gain = small_ref[taps + 1 : taps + 2]
    for i, (a_ref, b_ref) in enumerate(((one_ref, got_one_ref), (two_ref, got_two_ref))):
        part = slice(i * half, (i + 1) * half)
        grad = a_ref[...].astype(F32) + b_ref[...].astype(F32)
        middle = middle_ref[part]
        scale = rms_scale(middle)
        normed = middle * scale
        total = total + jnp.sum(grad * normed, axis=0, keepdims=True)
        grad_middle = cot_ref[part].astype(F32) + norm_back(grad, normed, scale, gain)
        grad_middle_ref[part] = grad_middle
        low_ref[part] = grad_middle.astype(LOW)
    gain_ref[...] = total
    grad_y = dot(low_ref[...], w_ref[...], 1, 1)
    grad_c_ref[...] = (grad_y * conv_ref[...]).astype(LOW)
    grad_conv_ref[...] = grad_y * c_ref[...]


def mixer_back_call(parts, cot, middle, small, out_w, conv, c_part):
    rows, width = cot.shape
    half = rows // 2
    (one, got_one), (two, got_two) = parts
    f32 = jax.ShapeDtypeStruct((rows, width), F32)
    low = jax.ShapeDtypeStruct((rows, width), LOW)
    whole = lambda shape: pl.BlockSpec(shape, lambda i: (0, 0))
    piece = whole((half, width))
    return pl.pallas_call(
        mixer_back_kernel,
        grid=(1,),
        in_specs=[piece] * 4
        + [whole(v.shape) for v in (cot, middle, small, out_w, conv, c_part)],
        out_specs=[whole((rows, width))] * 4 + [whole((1, width))],
        out_shape=[f32, low, low, f32, jax.ShapeDtypeStruct((1, width), F32)],
        cost_estimate=pl.CostEstimate(
            flops=2 * rows * width * width, bytes_accessed=30 * rows * width, transcendentals=0
        ),
        compiler_params=params(),
        name="mixer_back",
    )(one, got_one, two, got_two, cot, middle, small, out_w, conv, c_part)


def early_kernel(kept_one, kept_two, me_ref, in_ref, grad_c_ref, mixed_ref, low_ref, *refs):
    keep_one, send_one, keep_two, send_two, w_one, w_two, sems = refs
    w_one[...] = dot(in_ref[...], grad_c_ref[...], 0, 0, LOW)
    copies = place_rows(me_ref[0], kept_one, w_one, keep_one, send_one, sems.at[0])
    w_two[...] = dot(mixed_ref[...], low_ref[...], 0, 0, LOW)
    copies += place_rows(me_ref[0], kept_two, w_two, keep_two, send_two, sems.at[1])
    for copy in copies:
        copy.wait()


def weight_grads(kept_one, width):
    part = jax.ShapeDtypeStruct((width // 2, width), LOW)
    return [part] * 4, [
        pltpu.VMEM((width, width), LOW),
        pltpu.VMEM((width, width), LOW),
        pltpu.SemaphoreType.DMA((2, len(kept_one), 2)),
    ]


def early_call(me, kepts, mixer_in, grad_c, mixed, low):
    rows, width = mixer_in.shape
    shapes, scratch = weight_grads(kepts[0], width)
    return pl.pallas_call(
        functools.partial(early_kernel, *kepts),
        in_specs=[SMEM] + [VMEM] * 4,
        out_specs=[ANY] * 4,
        out_shape=shapes,
        scratch_shapes=scratch,
        cost_estimate=pl.CostEstimate(
            flops=4 * rows * width * width, bytes_accessed=8 * width * width, transcendentals=0
        ),
        compiler_params=params(),
        name="early_grads",
    )(me, mixer_in, grad_c, mixed, low)


def late_kernel(
    kept_one, kept_two, seqs, me_ref, conv_grad_ref, head_ref, small_ref, bx_ref, tail_ref, b_ref,
    x_ref, in_ref, gb_ref, gx_ref, tap_ref, *refs,
):
    keep_one, send_one, keep_two, send_two, ext, ext_grad, w_one, w_two, sems = refs
    span = bx_ref.shape[0] // seqs
    halo = tail_ref.shape[1]
    taps = halo + 1
    sums = [0.0] * taps
    for s in range(seqs):
        part = pl.ds(s * span, span)
        grad = conv_grad_ref[part]
        ext[pl.ds(8, span)] = bx_ref[part].astype(F32)
        ext[8 - halo : 8] = tail_ref[s].astype(F32)
        ext_grad[pl.ds(0, span)] = grad
        ext_grad[span : span + halo] = head_ref[s].astype(F32)
        grad_bx = jnp.zeros_like(grad)
        for j in range(taps):
            grad_bx = grad_bx + small_ref[j : j + 1] * ext_grad[pl.ds(halo - j, span)]
            sums[j] = sums[j] + jnp.sum(
                grad * ext[pl.ds(8 - halo + j, span)], axis=0, keepdims=True
            )
        gb_ref[part] = (grad_bx * x_ref[part]).astype(LOW)
        gx_ref[part] = (grad_bx * b_ref[part]).astype(LOW)
    tap_ref[...] = jnp.concatenate(sums + [jnp.zeros_like(sums[0])] * (8 - taps), axis=0)
    w_one[...] = dot(in_ref[...], gb_ref[...], 0, 0, LOW)
    copies = place_rows(me_ref[0], kept_one, w_one, keep_one, send_one, sems.at[0])
    w_two[...] = dot(in_ref[...], gx_ref[...], 0, 0, LOW)
    copies += place_rows(me_ref[0], kept_two, w_two, keep_two, send_two, sems.at[1])
    for copy in copies:
        copy.wait()


def late_call(me, kepts, grad_conv, head, small, bx, tail, b_part, x_part, mixer_in):
    rows, width = mixer_in.shape
    seqs = tail.shape[0]
    shapes, scratch = weight_grads(kepts[0], width)
    low = jax.ShapeDtypeStruct((rows, width), LOW)
    line = pltpu.VMEM((rows // seqs + 8, width), F32)
    return pl.pallas_call(
        functools.partial(late_kernel, *kepts, seqs),
        in_specs=[SMEM] + [VMEM] * 8,
        out_specs=[VMEM] * 3 + [ANY] * 4,
        out_shape=[low, low, jax.ShapeDtypeStruct((8, width), F32)] + shapes,
        scratch_shapes=[line, line] + scratch,
        cost_estimate=pl.CostEstimate(
            flops=4 * rows * width * width, bytes_accessed=20 * width * width, transcendentals=0
        ),
        compiler_params=params(),
        name="late_grads",
    )(me, grad_conv, head, small, bx, tail, b_part, x_part, mixer_in)


def input_kernel(gb_ref, gc_ref, gx_ref, w_ref, x_ref, grad_middle_ref, small_ref, out_ref, gain_ref):
    width = x_ref.shape[1]
    grad = dot(gb_ref[...], w_ref[:, :width], 1, 1)
    grad = grad + dot(gc_ref[...], w_ref[:, width : 2 * width], 1, 1)
    grad = grad + dot(gx_ref[...], w_ref[:, 2 * width : 3 * width], 1, 1)
    x = x_ref[...].astype(F32)
    scale = rms_scale(x)
    normed = x * scale
    taps = 3
    gain_ref[...] = jnp.sum(grad * normed, axis=0, keepdims=True)
    out_ref[...] = (
        grad_middle_ref[...] + norm_back(grad, normed, scale, small_ref[taps : taps + 1])
    ).astype(LOW)


def input_call(gb, gc, gx, in_w, x, grad_middle, small):
    rows, width = x.shape
    return pl.pallas_call(
        input_kernel,
        in_specs=[VMEM] * 7,
        out_specs=[VMEM] * 2,
        out_shape=[
            jax.ShapeDtypeStruct((rows, width), LOW),
            jax.ShapeDtypeStruct((1, width), F32),
        ],
        cost_estimate=pl.CostEstimate(
            flops=6 * rows * width * width, bytes_accessed=12 * width * width, transcendentals=0
        ),
        compiler_params=params(),
        name="input_grads",
    )(gb, gc, gx, in_w, x, grad_middle, small)


def shards(
    block_input,
    cotangent,
    in_proj,
    out_proj,
    gate_proj,
    up_proj,
    down_proj,
    conv_weight,
    mixer_gain,
    ffn_gain,
):
    nd, ns = lax.axis_size("dp"), lax.axis_size("seq")
    chips = nd // 2
    me = lax.axis_index("dp")
    me_vec = me.astype(jnp.int32).reshape(1)
    chip, core = me // 2, me % 2
    bits = []
    while 2 ** len(bits) < chips:
        bits.append(2 << len(bits))
    seqs, span, width = block_input.shape
    rows_all = seqs * span
    half = rows_all // 2
    own_rows = in_proj.shape[0]
    taps = conv_weight.shape[1]
    halo = taps - 1
    slice_ff = gate_proj.shape[1] // chips
    orders = (bits, bits[::-1])

    out_grad = cotangent.reshape(rows_all, width)

    def gathered(one, two):
        found = [spread(v, o) for v, o in zip((one, two), orders)]
        sets = [level_sets(order) for order in orders]
        return [
            [found[c][j] for c in (0, 1) for j in sets[c][level]] for level in range(len(sets[0]))
        ]

    grads_pieces = gathered(out_grad[:half], out_grad[half:])

    small = jnp.concatenate([conv_weight, mixer_gain[:, None], ffn_gain[:, None]], axis=1)
    small = jnp.pad(small, ((0, 0), (0, SMALL - small.shape[1])))
    packed = jnp.concatenate([in_proj, small, out_proj], axis=1)
    packed = lax.all_gather(packed, "seq", axis=0, tiled=True)
    packed = after(packed, *grads_pieces[0])
    cut, end = 3 * width // 2, 3 * width + SMALL
    order_one = orders[0] + [1]
    order_two = orders[1] + [1]
    blocks_one = spread(packed[:, :cut], order_one)
    blocks_two = spread(packed[:, cut:end], order_two)
    out_blocks = spread(packed[:, end:], order_one)

    def columns_for(mask):
        at = (chip ^ mask) * slice_ff
        return jnp.concatenate(
            [lax.dynamic_slice(w, (0, at), (own_rows, slice_ff)) for w in (gate_proj, up_proj)],
            axis=1,
        )

    gate_up = jnp.stack([columns_for(0)] + [swap(columns_for(k), 2 * k) for k in range(1, chips)])
    gate_up = xor_order(gate_up, chip)
    gate_up = lax.all_gather(gate_up, "seq", axis=0, tiled=False)
    down = lax.all_gather(down_proj, "seq", axis=0, tiled=True)

    x_low = block_input.reshape(rows_all, width)
    x_low = after(x_low, *[p for level in grads_pieces[1:] for p in level])
    in_w, small, mixer_in, b_part, x_part, bx_value = mixer_in_call(
        me_vec, x_low, blocks_one, blocks_two
    )
    bx_seq = bx_value.reshape(seqs, span, width)
    tail_rows = along_seq(bx_seq[:, span - halo :, :], 1)
    c_part = dot(mixer_in, in_w[:, width : 2 * width], 1, 0)
    gate_up = after(gate_up, c_part)
    other = swap(gate_up, 1)
    out_w, conv_flat, mixed_y, middle, ffn_one, ffn_two = mixer_out_call(
        me_vec, x_low, bx_value, tail_rows, c_part, small, out_blocks
    )
    gate_up, other, _ = lax.optimization_barrier((gate_up, other, ffn_one))
    gate_up, other = (v.transpose(1, 0, 2, 3) for v in (gate_up, other))
    gate_up = jnp.stack(
        [jnp.where(core == 0, gate_up, other), jnp.where(core == 0, other, gate_up)], axis=1
    ).reshape(width, 2 * slice_ff)
    down = after(down, ffn_two)
    other = swap(down, 1)
    down = jnp.concatenate(
        [jnp.where(core == 0, down, other), jnp.where(core == 0, other, down)], axis=0
    )

    acts_pieces = gathered(ffn_one, ffn_two)
    total = chips * rows_all
    kept, base, partial = [], 0, []
    for acts, grads in zip(acts_pieces, grads_pieces):
        *kept, na, nb, da, db = ffn_call(acts, grads, gate_up, down, kept, base, total)
        base += len(acts) * half
        partial.append(((na, nb), (da, db)))
    hidden, grad_gu, acts_all, grads_all = kept

    def first_steps(which, levels=None):
        found = []
        for color, order in enumerate(orders):
            levels = [p[which][color] for p in partial]
            for level in range(len(order) - 1, 0, -1):
                got = swap(levels[level], order[level])
                found.append(got)
        return found

    def sums(which, gots):
        result, place = [], 0
        for color, order in enumerate(orders):
            levels = [p[which][color] for p in partial]
            for level in range(len(order) - 1, 0, -1):
                got, at = gots[place], 0
                place += 1
                for i in range(level):
                    n = levels[i].shape[0]
                    levels[i] = added(levels[i], got[at : at + n])
                    at += n
            got = swap(levels[0][half:], order[0])
            result.append((levels[0], got))
        return result

    gots = first_steps(0)

    grad_gate_up = dot(acts_all, grad_gu, 0, 0, LOW)
    grad_gate_up = grad_gate_up.reshape(chips, 2, ns, own_rows, 2 * slice_ff)
    keep_gu = lax.dynamic_index_in_dim(grad_gate_up, core, 1, keepdims=False)
    send = lax.dynamic_index_in_dim(grad_gate_up, 1 - core, 1, keepdims=False)
    got_gu = swap(send, 1)
    grad_down = dot(hidden, grads_all, 0, 0, LOW)
    grad_down = grad_down.reshape(2, slice_ff // 2, width)
    keep_down = lax.dynamic_index_in_dim(grad_down, core, 0, keepdims=False)
    send = lax.dynamic_index_in_dim(grad_down, 1 - core, 0, keepdims=False)
    got_down = swap(send, 1)

    *gots, _ = lax.optimization_barrier((*gots, send))
    norm_parts = sums(0, gots)
    total = added(keep_gu, got_gu).transpose(1, 0, 2, 3)
    total_down = added(keep_down, got_down)
    norm_parts, total, total_down, partial = lax.optimization_barrier(
        (norm_parts, total, total_down, partial)
    )
    down_gots = first_steps(1)
    total = lax.psum_scatter(total, "seq", scatter_dimension=0, tiled=False)
    grad_down_w = lax.psum_scatter(total_down, "seq", scatter_dimension=0, tiled=True).astype(F32)

    grad_middle, grad_mid_low, grad_c, grad_conv, grad_ffn_gain = mixer_back_call(
        norm_parts, out_grad, middle, small, out_w, conv_flat, c_part
    )
    head_rows = along_seq(
        grad_conv.reshape(seqs, span, width)[:, :halo, :].astype(LOW), -1
    )
    kepts = [kept_order(order) for order in orders]
    early = early_call(me_vec, kepts, mixer_in, grad_c, mixed_y, grad_mid_low)

    def core_step(parts):
        found = []
        for color in (0, 1):
            found.append(swap(parts[2 * color + 1], 1))
        return found

    early_gots = core_step(early)
    early_gots, down_gots = lax.optimization_barrier((early_gots, down_gots))
    down_parts = sums(1, down_gots)
    grad_b, grad_x, tap_grads, *late = late_call(
        me_vec, kepts, grad_conv, head_rows, small, bx_value, tail_rows, b_part, x_part, mixer_in
    )
    late_gots = core_step(late)

    def chip_steps(parts, gots, before):
        result = []
        for color, order in enumerate(orders):
            held = added(parts[2 * color], gots[color])
            for mask in order[::-1]:
                held = added(*halve(held, mask))
            result.append(held)
        held = after(jnp.concatenate(result, axis=1), before)
        return lax.psum_scatter(held, "seq", scatter_dimension=0, tiled=True).astype(F32)

    early_mine = chip_steps(early, early_gots, total)
    late_mine = chip_steps(late, late_gots, grad_down_w)
    input_grad, grad_mix_gain = input_call(
        after(grad_b, total, down_parts), grad_c, grad_x, in_w, x_low, grad_middle, small
    )
    input_grad = input_grad.reshape(seqs, span, width)

    down_term = jnp.concatenate(
        [kept[:half].astype(F32) + got.astype(F32) for kept, got in down_parts], axis=0
    )
    block_output = (middle + down_term).astype(LOW).reshape(seqs, span, width)

    def rows_for(mask):
        return lax.dynamic_index_in_dim(total, chip ^ mask, 0, keepdims=False)

    owned = jnp.stack([rows_for(0)] + [swap(rows_for(k), 2 * k) for k in range(1, chips)])
    owned = xor_order(owned, chip).astype(F32).transpose(1, 0, 2)
    grad_gate_w = owned[:, :, :slice_ff].reshape(own_rows, chips * slice_ff)
    grad_up_w = owned[:, :, slice_ff:].reshape(own_rows, chips * slice_ff)

    vectors = jnp.concatenate(
        [tap_grads[:taps], grad_mix_gain, grad_ffn_gain, jnp.zeros((6 - taps, width), F32)], axis=0
    )
    mask = 1
    while mask < nd:
        vectors = vectors + swap(vectors, mask)
        mask *= 2
    mask = 1
    while mask < ns:
        pairs = [(source, source ^ mask) for source in range(ns)]
        vectors = vectors + lax.ppermute(vectors, "seq", pairs)
        mask *= 2
    vectors = lax.dynamic_slice(
        vectors, (0, (me * ns + lax.axis_index("seq")) * own_rows), (8, own_rows)
    )
    return (
        block_output,
        input_grad,
        jnp.concatenate([late_mine[:, :width], early_mine[:, :width], late_mine[:, width:]], axis=1),
        early_mine[:, width:],
        grad_gate_w,
        grad_up_w,
        grad_down_w,
        vectors[:taps].T,
        vectors[taps],
        vectors[taps + 1],
    )


def solution(mesh):
    rows, vector = P(("dp", "seq"), None), P(("dp", "seq"))
    acts = P("dp", "seq", None)
    in_specs = (acts, acts) + (rows,) * 6 + (vector,) * 2
    out_specs = (acts, acts) + (rows,) * 6 + (vector,) * 2

    return jax.shard_map(shards, mesh=mesh, in_specs=in_specs, out_specs=out_specs, check_vma=False)
```
